128 devices in a mesh: seq: 32 (over y, z, core), head: 4 (over x).
Axes of the slice: x: 4, y: 4, z: 4, core: 2. Of those that a mesh axis runs over, the one named last changes fastest.
Arguments:
- vision: bfloat16 [65536, 7680], P(('seq', 'head')), may hold values from -6 to 6
- w_key: bfloat16 [7680, 512], replicated, may hold values from -0.0625 to 0.0625
- w_value: bfloat16 [7680, 512], replicated, may hold values from -0.0625 to 0.0625
- queries: bfloat16 [256, 4096], P('seq', 'head'), may hold values from -240 to 240
- w_out: bfloat16 [4096, 8192], P('head', 'seq'), may hold values from -0.09375 to 0.09375
Outputs:
- mixed: bfloat16 [256, 8192], P('head', 'seq')
The draws below stay inside these ranges and needn't reach their ends.
All inputs are finite; a program needn't handle non-finite values.
Results may differ from the reference program's by a relative error of at most 0.03.
Values may be sent and summed in bfloat16 or wider, within the bound.
No kernel may reach another device: no remote copies, remote signals or barrier semaphores. Data moves between devices by JAX's collectives and lax.ppermute only.
A program may use at most 128 MiB of HBM per device.

```python
import jax
import jax.numpy as jnp
from jax import lax

VD = 7680
D = 8192
HD = 128
QH = 32
KV = 4
TEXT = 256
VTOK = 65536
N_SEQ = 32


def draw_queries(key, part):
    first_key = jax.random.fold_in(key, 11)
    base = jnp.clip(jax.random.normal(first_key, (TEXT, QH * HD), jnp.float32), -4.0, 4.0)
    result = base * 3.0
    return result.astype(jnp.bfloat16)


def steps_of(key, dims, shards, smallest, high):
    loudness, own = 1.0, jax.random.fold_in(key, 6)
    for axis_at, shards_of in shards:
        steps = jnp.exp(jax.random.uniform(jax.random.fold_in(own, axis_at), (shards_of,), jnp.float32, smallest / len(shards), high / len(shards)))
        loudness = loudness * jnp.repeat(steps, dims[axis_at] // shards_of).reshape([-1 if axis == axis_at else 1 for axis in range(len(dims))])
    return loudness


def noise(key, dims, deviation, bound, cuts=(), kind=jnp.bfloat16):
    entries = jax.random.normal(key, dims, jnp.float32) * deviation
    if len(cuts) > 0:
        entries = steps_of(key, dims, cuts, -0.22, 0.18) * entries
    return jnp.clip(entries, min=-bound, max=bound).astype(kind)


def setup_inputs(seed: int = 0) -> dict:
    seeds = jax.random.split(jax.random.key(seed), 6)
    vision = noise(seeds[0], (VTOK, VD), 1.0, 6.0, ((0, 128),))
    w_key = noise(seeds[1], (VD, KV * HD), VD ** -0.5, 0.0625)
    w_value = noise(seeds[2], (VD, KV * HD), VD ** -0.5, 0.0625)
    queries = draw_queries(jax.random.fold_in(seeds[5], 71), 0)
    w_out = noise(seeds[4], (QH * HD, D), (QH * HD) ** -0.5, 0.09375, ((0, 4), (1, 32)))
    return {"vision": vision, "w_key": w_key, "w_value": w_value, "queries": queries, "w_out": w_out}


def reference(vision, w_key, w_value, queries, w_out):
    keys = jnp.dot(vision, w_key, preferred_element_type=jnp.float32).astype(jnp.bfloat16)
    values = jnp.dot(vision, w_value, preferred_element_type=jnp.float32).astype(jnp.bfloat16)
    keys = lax.optimization_barrier(keys)
    values = lax.optimization_barrier(values)
    block_len = VTOK // N_SEQ
    group_size = QH // KV
    key_blocks = keys.reshape(N_SEQ, block_len, KV, HD)
    value_blocks = values.reshape(N_SEQ, block_len, KV, HD)
    grouped = queries.astype(jnp.float32).reshape(TEXT, KV, group_size, HD)

    def one_block(pair):
        key_part, value_part = pair
        scores = jnp.einsum("tkgd,nkd->kgtn", grouped, key_part.astype(jnp.float32)) * (HD ** -0.5)
        maxima = jnp.max(scores, axis=-1)
        powers = jnp.exp(scores - maxima[..., None])
        totals = jnp.sum(powers, axis=-1)
        rounded = lax.optimization_barrier(powers.astype(jnp.bfloat16))
        partial_value = jnp.einsum("kgtn,nkd->tkgd", rounded.astype(jnp.float32), value_part.astype(jnp.float32))
        partial_value = partial_value.reshape(TEXT, QH * HD)
        maxima = maxima.transpose(2, 0, 1).reshape(TEXT, QH)
        totals = totals.transpose(2, 0, 1).reshape(TEXT, QH)
        return maxima, totals, partial_value

    block_max, block_sum, block_out = lax.map(one_block, (key_blocks, value_blocks))
    row_max = jnp.max(block_max, axis=0)
    factor = jnp.exp(block_max - row_max[None])
    denom = jnp.sum(block_sum * factor, axis=0)
    numer = jnp.sum(block_out.reshape(N_SEQ, TEXT, QH, HD) * factor[..., None], axis=0)
    attended = (numer / denom[..., None]).reshape(TEXT, QH * HD).astype(jnp.bfloat16)
    return jnp.dot(attended, w_out, preferred_element_type=jnp.float32).astype(jnp.bfloat16)
```

```python
import math

import jax
import jax.numpy as jnp
from jax import lax
from jax.experimental import pallas as pl
from jax.experimental.pallas import tpu as pltpu
from jax.sharding import Mesh, PartitionSpec as P

HD = 128
HEADS = 8
RPD = 8
PEERS = 16
ROWS = PEERS * RPD
TOK = 512
BLK = HEADS + 1
EXP2_SCALE = HD ** -0.5 * math.log2(math.e)
VMEM = pl.BlockSpec(memory_space=pltpu.VMEM)
ANY = pl.BlockSpec(memory_space=pl.ANY)
SMEM = pl.BlockSpec(memory_space=pltpu.SMEM)
YZ = ("y", "z")
CHUNKS = (768,) * 10
AHEAD = 2


def project_kernel(x, wk, wv, ko, vo, xb, wkb, wvb, acck, accv, sems):
    offsets = [sum(CHUNKS[:i]) for i in range(len(CHUNKS))]
    copies = []
    for i, (at, size) in enumerate(zip(offsets, CHUNKS)):
        part = pl.ds(at, size)
        copies.append(
            [
                pltpu.make_async_copy(x.at[:, part], xb.at[:, part], sems.at[0, i]),
                pltpu.make_async_copy(wk.at[part, :], wkb.at[part, :], sems.at[1, i]),
                pltpu.make_async_copy(wv.at[part, :], wvb.at[part, :], sems.at[2, i]),
            ]
        )
    for i in range(AHEAD):
        for copy in copies[i]:
            copy.start()
    last = len(CHUNKS) - 1
    for i, (at, size) in enumerate(zip(offsets, CHUNKS)):
        for copy in copies[i]:
            copy.wait()
        if i + AHEAD <= last:
            for copy in copies[i + AHEAD]:
                copy.start()
        for w, acc, out in ((wkb, acck, ko), (wvb, accv, vo)):
            part = jnp.dot(
                xb[:, at : at + size], w[at : at + size, :], preferred_element_type=jnp.float32
            )
            if i > 0:
                part = acc[...] + part
            if i < last:
                acc[...] = part
            else:
                for h in range(4):
                    out[h] = part[:, h * HD : (h + 1) * HD].astype(jnp.bfloat16)


def project(vision, w_key, w_value):
    rows, width = vision.shape
    cols = w_key.shape[1]
    out = jax.ShapeDtypeStruct((4, rows, HD), jnp.bfloat16)
    return pl.pallas_call(
        project_kernel,
        in_specs=[ANY] * 3,
        out_specs=[VMEM] * 2,
        out_shape=[out] * 2,
        scratch_shapes=[
            pltpu.VMEM((rows, width), jnp.bfloat16),
            pltpu.VMEM((width, cols), jnp.bfloat16),
            pltpu.VMEM((width, cols), jnp.bfloat16),
            pltpu.VMEM((rows, cols), jnp.float32),
            pltpu.VMEM((rows, cols), jnp.float32),
            pltpu.SemaphoreType.DMA((3, len(CHUNKS))),
        ],
        name="project",
    )(vision, w_key, w_value)


def attend_kernel(q, k1, v1, k2, v2, out):
    tokens = k1.shape[0]
    sub = lax.broadcasted_iota(jnp.int32, (ROWS, HD), 0) % RPD
    lane = lax.broadcasted_iota(jnp.int32, (ROWS, HD), 1)
    stats = jnp.zeros((ROWS, HD), jnp.float32)
    contract = (((1,), (1,)), ((), ()))
    ones = jnp.ones((tokens, HD), jnp.bfloat16)
    for h in range(HEADS):
        qh = q[:, h * HD : (h + 1) * HD]
        s1 = lax.dot_general(qh, k1[...], contract, preferred_element_type=jnp.float32)
        s2 = lax.dot_general(qh, k2[...], contract, preferred_element_type=jnp.float32)
        top = jnp.maximum(
            jnp.max(s1, axis=1, keepdims=True), jnp.max(s2, axis=1, keepdims=True)
        )
        p1 = jnp.exp2((s1 - top) * EXP2_SCALE).astype(jnp.bfloat16)
        p2 = jnp.exp2((s2 - top) * EXP2_SCALE).astype(jnp.bfloat16)
        acc = jnp.dot(
            p1, jnp.concatenate([v1[...], ones], axis=1), preferred_element_type=jnp.float32
        ) + jnp.dot(
            p2, jnp.concatenate([v2[...], ones], axis=1), preferred_element_type=jnp.float32
        )
        out[:, h] = acc[:, :HD].reshape(PEERS, RPD, HD).astype(jnp.bfloat16)
        stats = jnp.where(lane == h * RPD + sub, top, stats)
        stats = jnp.where(lane == HD // 2 + h * RPD + sub, acc[:, HD:], stats)
    mine = jnp.sum(stats.reshape(PEERS, RPD, HD), axis=1, keepdims=True)
    high = mine.astype(jnp.bfloat16).astype(jnp.float32)
    rest = mine - high
    mid = rest.astype(jnp.bfloat16).astype(jnp.float32)
    low = rest - mid
    place = lax.broadcasted_iota(jnp.int32, (PEERS, RPD, HD), 1)
    tile = jnp.where(
        place == 0, high, jnp.where(place == 1, mid, jnp.where(place == 2, low, 0.0))
    )
    out[:, HEADS] = tile.astype(jnp.bfloat16)


def attend(q, k1, v1, k2, v2):
    return pl.pallas_call(
        attend_kernel,
        in_specs=[VMEM] * 5,
        out_specs=VMEM,
        out_shape=jax.ShapeDtypeStruct((PEERS, BLK, RPD, HD), jnp.bfloat16),
        name="attend",
    )(q, k1, v1, k2, v2)


def combine_kernel(parts, out):
    half = HD // 2
    tile = parts[:, HEADS].astype(jnp.float32)
    stats = jnp.sum(tile, axis=1)
    maxima = stats[:, :half]
    sums = stats[:, half:]
    top = jnp.max(maxima, axis=0, keepdims=True)
    factor = jnp.exp2((maxima - top) * EXP2_SCALE)
    denom = jnp.sum(factor * sums, axis=0, keepdims=True)
    weight = (factor / denom).T
    total = jnp.zeros((HEADS * RPD, HD), jnp.float32)
    for s in range(PEERS):
        block = parts[s, :HEADS].astype(jnp.float32).reshape(HEADS * RPD, HD)
        total = total + block * weight[:, s : s + 1]
    total = total.reshape(HEADS, RPD, HD)
    row = jnp.concatenate([total[h] for h in range(HEADS)], axis=1).astype(jnp.bfloat16)
    for s in range(PEERS):
        out[s] = row


def combine(parts):
    return pl.pallas_call(
        combine_kernel,
        in_specs=[VMEM],
        out_specs=VMEM,
        out_shape=jax.ShapeDtypeStruct((PEERS, RPD, HEADS * HD), jnp.bfloat16),
        name="combine",
    )(parts)


def mix_kernel(core, own, other, w, out):
    cols = w.shape[1]
    mine = jnp.dot(own[...], w[...], preferred_element_type=jnp.float32)
    theirs = jnp.dot(other[...], w[...], preferred_element_type=jnp.float32)
    mine = mine.reshape(PEERS, 1, RPD, cols)
    theirs = theirs.reshape(PEERS, 1, RPD, cols)
    first = core[0] == 0
    pair = jnp.concatenate(
        [jnp.where(first, mine, theirs), jnp.where(first, theirs, mine)], axis=1
    )
    out[...] = pair.reshape(2 * ROWS, cols).astype(jnp.bfloat16)


def mix(core, own, other, w):
    return pl.pallas_call(
        mix_kernel,
        in_specs=[SMEM, VMEM, VMEM, VMEM],
        out_specs=VMEM,
        out_shape=jax.ShapeDtypeStruct((2 * ROWS, w.shape[1]), jnp.bfloat16),
        name="mix",
    )(core, own, other, w)


def swap_cores(x):
    return lax.ppermute(x, "core", [(0, 1), (1, 0)])


def exchange(x, axes):
    return lax.all_to_all(x, axes, split_axis=0, concat_axis=0, tiled=True)


def shards(vision, w_key, w_value, queries, w_out):
    rows = exchange(jnp.tile(queries, (PEERS, 1)), YZ)
    keys, values = project(vision, w_key, w_value)
    k1 = exchange(keys, "head").reshape(-1, HD)
    v1 = exchange(values, "head").reshape(-1, HD)
    k2 = swap_cores(k1)
    v2 = swap_cores(v1)
    parts = exchange(attend(rows, k1, v1, k2, v2), YZ)
    own = exchange(combine(parts), YZ).reshape(ROWS, HEADS * HD)
    other = swap_cores(own)
    core = lax.axis_index("core").astype(jnp.int32).reshape(1)
    partial = mix(core, own, other, w_out)
    shares = exchange(partial, "head").reshape(4, -1, partial.shape[1])
    return jnp.sum(shares.astype(jnp.float32), axis=0).astype(jnp.bfloat16)


def solution(mesh):
    fine = Mesh(mesh.devices.reshape(4, 4, 2, 4), ("y", "z", "core", "head"))
    seq = ("y", "z", "core")
    placed = (P(seq + ("head",), None), P(), P(), P(seq, "head"), P("head", seq))
    return jax.shard_map(
        shards, mesh=fine, in_specs=placed, out_specs=P("head", seq), check_vma=False
    )
```

```python
import math

import jax
import jax.numpy as jnp
from jax import lax
from jax.experimental import pallas as pl
from jax.experimental.pallas import tpu as pltpu
from jax.sharding import Mesh, PartitionSpec as P


HD = 128
GROUPS = 4
HEADS = 8
RPD = 8
YZ_SIZE = 16
PEERS = YZ_SIZE * GROUPS
ROWS = YZ_SIZE * RPD
BLK = HEADS + 1
STACK = 2
EXP2_SCALE = HD ** -0.5 * math.log2(math.e)
VMEM = pl.BlockSpec(memory_space=pltpu.VMEM)
HBM = pl.BlockSpec(memory_space=pltpu.HBM)
SMEM = pl.BlockSpec(memory_space=pltpu.SMEM)
YZ = ("y", "z")
YZX = ("y", "z", "head")
CHUNKS = (768,) * 10
AHEAD = 3


def limit(mib):
    return pltpu.CompilerParams(vmem_limit_bytes=mib * 1024 * 1024)


def project_kernel(x, wk, wv, out, xb, wkb, wvb, acc, sems):
    offsets = [sum(CHUNKS[:i]) for i in range(len(CHUNKS))]
    copies = []
    for i, (at, size) in enumerate(zip(offsets, CHUNKS)):
        part = pl.ds(at, size)
        copies.append(
            [
                pltpu.make_async_copy(x.at[:, part], xb.at[:, part], sems.at[0, i]),
                pltpu.make_async_copy(wk.at[part, :], wkb.at[part, :], sems.at[1, i]),
                pltpu.make_async_copy(wv.at[part, :], wvb.at[part, :], sems.at[2, i]),
            ]
        )
    for i in range(AHEAD):
        for copy in copies[i]:
            copy.start()
    last = len(CHUNKS) - 1
    for i, (at, size) in enumerate(zip(offsets, CHUNKS)):
        for copy in copies[i]:
            copy.wait()
        if i + AHEAD <= last:
            for copy in copies[i + AHEAD]:
                copy.start()
        for j, w in enumerate((wkb, wvb)):
            part = jnp.dot(
                xb[:, at : at + size], w[at : at + size, :], preferred_element_type=jnp.float32
            )
            if i > 0:
                part = acc[j] + part
            if i < last:
                acc[j] = part
            else:
                for g in range(GROUPS):
                    out[g, j] = part[:, g * HD : (g + 1) * HD].astype(jnp.bfloat16)


def project(vision, w_key, w_value):
    rows, width = vision.shape
    cols = w_key.shape[1]
    return pl.pallas_call(
        project_kernel,
        in_specs=[HBM] * 3,
        out_specs=VMEM,
        out_shape=jax.ShapeDtypeStruct((GROUPS, 2, rows, HD), jnp.bfloat16),
        scratch_shapes=[
            pltpu.VMEM((rows, width), jnp.bfloat16),
            pltpu.VMEM((width, cols), jnp.bfloat16),
            pltpu.VMEM((width, cols), jnp.bfloat16),
            pltpu.VMEM((2, rows, cols), jnp.float32),
            pltpu.SemaphoreType.DMA((3, len(CHUNKS))),
        ],
        compiler_params=limit(56),
        name="project",
    )(vision, w_key, w_value)


def split_stats(stats):
    mine = jnp.sum(stats.reshape(YZ_SIZE, RPD, HD), axis=1, keepdims=True)
    high = mine.astype(jnp.bfloat16).astype(jnp.float32)
    rest = mine - high
    mid = rest.astype(jnp.bfloat16).astype(jnp.float32)
    low = rest - mid
    place = lax.broadcasted_iota(jnp.int32, (YZ_SIZE, RPD, HD), 1)
    tile = jnp.where(
        place == 0, high, jnp.where(place == 1, mid, jnp.where(place == 2, low, 0.0))
    )
    return tile.astype(jnp.bfloat16)


def peer_of(tile, group):
    block, part = divmod(tile, GROUPS)
    slot = (group - block) % GROUPS
    return (part * GROUPS + slot) * GROUPS + block


def attend_kernel(q, kv1, kv2, out):
    tokens = kv1.shape[2]
    sub = lax.broadcasted_iota(jnp.int32, (ROWS, HD), 0) % RPD
    lane = lax.broadcasted_iota(jnp.int32, (ROWS, HD), 1)
    contract = (((1,), (1,)), ((), ()))
    ones = jnp.ones((tokens, HD), jnp.bfloat16)
    for g in range(GROUPS):
        stats = jnp.zeros((ROWS, HD), jnp.float32)
        v1 = jnp.concatenate([kv1[g, 1], ones], axis=1)
        v2 = jnp.concatenate([kv2[g, 1], ones], axis=1)
        for first in range(0, HEADS, STACK):
            qs = [
                q[:, g, :, h * HD : (h + 1) * HD].reshape(ROWS, HD)
                for h in range(first, first + STACK)
            ]
            qs = jnp.concatenate(qs, axis=0)
            s1 = lax.dot_general(qs, kv1[g, 0], contract, preferred_element_type=jnp.float32)
            s2 = lax.dot_general(qs, kv2[g, 0], contract, preferred_element_type=jnp.float32)
            top = jnp.max(jnp.maximum(s1, s2), axis=1, keepdims=True)
            p1 = jnp.exp2((s1 - top) * EXP2_SCALE).astype(jnp.bfloat16)
            p2 = jnp.exp2((s2 - top) * EXP2_SCALE).astype(jnp.bfloat16)
            acc = jnp.dot(p1, v1, preferred_element_type=jnp.float32) + jnp.dot(
                p2, v2, preferred_element_type=jnp.float32
            )
            for k in range(STACK):
                h = first + k
                mine = acc[k * ROWS : (k + 1) * ROWS]
                for t in range(YZ_SIZE):
                    out[peer_of(t, g), h] = mine[t * RPD : (t + 1) * RPD, :HD].astype(
                        jnp.bfloat16
                    )
                stats = jnp.where(
                    lane == h * RPD + sub, top[k * ROWS : (k + 1) * ROWS], stats
                )
                stats = jnp.where(lane == HD // 2 + h * RPD + sub, mine[:, HD:], stats)
        tiles = split_stats(stats)
        for t in range(YZ_SIZE):
            out[peer_of(t, g), HEADS] = tiles[t]


def attend(q, kv1, kv2):
    return pl.pallas_call(
        attend_kernel,
        in_specs=[VMEM] * 3,
        out_specs=VMEM,
        out_shape=jax.ShapeDtypeStruct((PEERS, BLK, RPD, HD), jnp.bfloat16),
        compiler_params=limit(32),
        name="attend",
    )(q, kv1, kv2)


def combine_kernel(parts, out):
    half = HD // 2
    tile = parts[:, HEADS].astype(jnp.float32)
    stats = jnp.sum(tile, axis=1)
    maxima = stats[:, :half]
    sums = stats[:, half:]
    top = jnp.max(maxima, axis=0, keepdims=True)
    factor = jnp.exp2((maxima - top) * EXP2_SCALE)
    denom = jnp.sum(factor * sums, axis=0, keepdims=True)
    weight = (factor / denom).T
    total = jnp.zeros((HEADS * RPD, HD), jnp.float32)
    for s in range(PEERS):
        block = parts[s, :HEADS].astype(jnp.float32).reshape(HEADS * RPD, HD)
        total = total + block * weight[:, s : s + 1]
    total = total.reshape(HEADS, RPD, HD)
    row = jnp.concatenate([total[h] for h in range(HEADS)], axis=1).astype(jnp.bfloat16)
    for s in range(YZ_SIZE):
        out[s] = row


def combine(parts):
    return pl.pallas_call(
        combine_kernel,
        in_specs=[VMEM],
        out_specs=VMEM,
        out_shape=jax.ShapeDtypeStruct((YZ_SIZE, RPD, HEADS * HD), jnp.bfloat16),
        compiler_params=limit(8),
        name="combine",
    )(parts)


def mix_kernel(core, own, other, w0, w1, w2, w3, out):
    cols = w0.shape[1]
    half = GROUPS * RPD
    total = jnp.zeros((2 * half, cols), jnp.float32)
    for slot, w in enumerate((w0, w1, w2, w3)):
        rows = jnp.concatenate(
            [own[:, slot].reshape(half, -1), other[:, slot].reshape(half, -1)], axis=0
        )
        total = total + jnp.dot(rows, w[...], preferred_element_type=jnp.float32)
    mine = total[:half].reshape(GROUPS, 1, RPD, cols)
    theirs = total[half:].reshape(GROUPS, 1, RPD, cols)
    first = core[0] == 0
    pair = jnp.concatenate(
        [jnp.where(first, mine, theirs), jnp.where(first, theirs, mine)], axis=1
    )
    out[...] = pair.reshape(2 * half, cols).astype(jnp.bfloat16)


def mix(core, own, other, shares):
    return pl.pallas_call(
        mix_kernel,
        in_specs=[SMEM] + [VMEM] * 6,
        out_specs=VMEM,
        out_shape=jax.ShapeDtypeStruct((2 * GROUPS * RPD, shares[0].shape[1]), jnp.bfloat16),
        compiler_params=limit(8),
        name="mix",
    )(core, own, other, *shares)


def swap_cores(x):
    return lax.ppermute(x, "core", [(0, 1), (1, 0)])


def exchange(x, axes):
    return lax.all_to_all(x, axes, split_axis=0, concat_axis=0, tiled=True)


def gather_share(w, ahead):
    return lax.ppermute(w, "head", [((i + ahead) % GROUPS, i) for i in range(GROUPS)])


def shards(vision, w_key, w_value, queries, w_out):
    copies = jnp.broadcast_to(queries[None], (PEERS,) + queries.shape)
    rows = exchange(copies, YZX).reshape(YZ_SIZE, GROUPS, RPD, -1)
    shares = [w_out] + [gather_share(w_out, k) for k in range(1, GROUPS)]
    kv1 = project(vision, w_key, w_value)
    kv2 = swap_cores(kv1)
    parts = exchange(attend(rows, kv1, kv2), YZX)
    own = exchange(combine(parts), YZ)
    other = swap_cores(own)
    core = lax.axis_index("core").astype(jnp.int32).reshape(1)
    shape = (GROUPS, GROUPS, RPD, -1)
    return mix(core, own.reshape(shape), other.reshape(shape), shares)


def solution(mesh):
    fine = Mesh(mesh.devices.reshape(4, 4, 2, 4), ("y", "z", "core", "head"))
    seq = ("y", "z", "core")
    placed = (P(seq + ("head",), None), P(), P(), P(seq, "head"), P("head", seq))
    return jax.shard_map(
        shards, mesh=fine, in_specs=placed, out_specs=P("head", seq), check_vma=False
    )
```

```python
import math

import jax
import jax.numpy as jnp
from jax import lax
from jax.experimental import pallas as pl
from jax.experimental.pallas import tpu as pltpu
from jax.sharding import Mesh, PartitionSpec as P


HD = 128
GROUPS = 4
HEADS = 8
RPD = 8
PEERS = 16
ROWS = PEERS * RPD
STACK = 2
BLK = HEADS + 1
EXP2_SCALE = HD ** -0.5 * math.log2(math.e)
VMEM = pl.BlockSpec(memory_space=pltpu.VMEM)
HBM = pl.BlockSpec(memory_space=pltpu.HBM)
SMEM = pl.BlockSpec(memory_space=pltpu.SMEM)
YZ = ("y", "z")
YZX = ("y", "z", "head")
CHUNKS = (768,) * 10
AHEAD = 3


def limit(mib):
    return pltpu.CompilerParams(vmem_limit_bytes=mib * 1024 * 1024)


def project_kernel(x, wk, wv, out, twin, xb, wkb, wvb, acc, sems):
    offsets = [sum(CHUNKS[:i]) for i in range(len(CHUNKS))]
    copies = []
    for i, (at, size) in enumerate(zip(offsets, CHUNKS)):
        part = pl.ds(at, size)
        copies.append(
            [
                pltpu.make_async_copy(x.at[:, part], xb.at[:, part], sems.at[0, i]),
                pltpu.make_async_copy(wk.at[part, :], wkb.at[part, :], sems.at[1, i]),
                pltpu.make_async_copy(wv.at[part, :], wvb.at[part, :], sems.at[2, i]),
            ]
        )
    for i in range(AHEAD):
        for copy in copies[i]:
            copy.start()
    last = len(CHUNKS) - 1
    for i, (at, size) in enumerate(zip(offsets, CHUNKS)):
        for copy in copies[i]:
            copy.wait()
        if i + AHEAD <= last:
            for copy in copies[i + AHEAD]:
                copy.start()
        for j, w in enumerate((wkb, wvb)):
            part = jnp.dot(
                xb[:, at : at + size], w[at : at + size, :], preferred_element_type=jnp.float32
            )
            if i > 0:
                part = acc[j] + part
            if i < last:
                acc[j] = part
            else:
                for g in range(GROUPS):
                    mine = part[:, g * HD : (g + 1) * HD].astype(jnp.bfloat16)
                    out[g, j] = mine
                    twin[g, j] = mine


def project(vision, w_key, w_value):
    rows, width = vision.shape
    cols = w_key.shape[1]
    return pl.pallas_call(
        project_kernel,
        in_specs=[HBM] * 3,
        out_specs=[VMEM] * 2,
        out_shape=[
            pltpu.VMEM((GROUPS, 2, rows, HD), jnp.bfloat16),
            jax.ShapeDtypeStruct((GROUPS, 2, rows, HD), jnp.bfloat16),
        ],
        scratch_shapes=[
            pltpu.VMEM((rows, width), jnp.bfloat16),
            pltpu.VMEM((width, cols), jnp.bfloat16),
            pltpu.VMEM((width, cols), jnp.bfloat16),
            pltpu.VMEM((2, rows, cols), jnp.float32),
            pltpu.SemaphoreType.DMA((3, len(CHUNKS))),
        ],
        compiler_params=limit(56),
        name="project",
    )(vision, w_key, w_value)


def stats_tile(stats):
    count = stats.shape[0]
    mine = stats.reshape(count, 1, HD)
    high = mine.astype(jnp.bfloat16).astype(jnp.float32)
    rest = mine - high
    mid = rest.astype(jnp.bfloat16).astype(jnp.float32)
    low = rest - mid
    place = lax.broadcasted_iota(jnp.int32, (count, RPD, HD), 1)
    tile = jnp.where(
        place == 0, high, jnp.where(place == 1, mid, jnp.where(place == 2, low, 0.0))
    )
    return tile.astype(jnp.bfloat16)


def attend_kernel(group, q, kv1, kv2, out):
    tokens = kv1.shape[2]
    row = lax.broadcasted_iota(jnp.int32, (ROWS, HD), 0)
    lane = lax.broadcasted_iota(jnp.int32, (ROWS, HD), 1)
    contract = (((1,), (1,)), ((), ()))
    ones = jnp.ones((tokens, HD), jnp.bfloat16)
    g = group[0]
    k1, k2 = kv1[g, 0], kv2[g, 0]
    v1 = jnp.concatenate([kv1[g, 1], ones], axis=1)
    v2 = jnp.concatenate([kv2[g, 1], ones], axis=1)
    stats = jnp.zeros((ROWS, HD), jnp.float32)
    for first in range(0, HEADS, STACK):
        qs = [
            q[:, g, :, h * HD : (h + 1) * HD].reshape(ROWS, HD)
            for h in range(first, first + STACK)
        ]
        qs = jnp.concatenate(qs, axis=0)
        s1 = lax.dot_general(qs, k1, contract, preferred_element_type=jnp.float32)
        s2 = lax.dot_general(qs, k2, contract, preferred_element_type=jnp.float32)
        top = jnp.max(jnp.maximum(s1, s2), axis=1, keepdims=True)
        p1 = jnp.exp2((s1 - top) * EXP2_SCALE).astype(jnp.bfloat16)
        p2 = jnp.exp2((s2 - top) * EXP2_SCALE).astype(jnp.bfloat16)
        acc = jnp.dot(p1, v1, preferred_element_type=jnp.float32) + jnp.dot(
            p2, v2, preferred_element_type=jnp.float32
        )
        for k in range(STACK):
            h = first + k
            mine = acc[k * ROWS : (k + 1) * ROWS]
            out[:, h] = mine[:, :HD].reshape(PEERS, RPD, HD).astype(jnp.bfloat16)
            pair = h * RPD + row % RPD
            stats = jnp.where(lane == pair, top[k * ROWS : (k + 1) * ROWS], stats)
            stats = jnp.where(lane == HD // 2 + pair, mine[:, HD:], stats)
    out[:, HEADS] = stats_tile(jnp.sum(stats.reshape(PEERS, RPD, HD), axis=1))


def attend(group, q, kv1, kv2):
    return pl.pallas_call(
        attend_kernel,
        in_specs=[SMEM] + [VMEM] * 3,
        out_specs=VMEM,
        out_shape=jax.ShapeDtypeStruct((PEERS, BLK, RPD, HD), jnp.bfloat16),
        compiler_params=limit(32),
        name="attend",
    )(group, q, kv1, kv2)


def read_stats(part):
    stats = jnp.sum(part[:, HEADS].astype(jnp.float32), axis=1)
    return stats[:, : HD // 2], stats[:, HD // 2 :]


def merge_kernel(*refs):
    sources, out = refs[:-1], refs[-1]
    stats = [read_stats(part) for part in sources]
    top = stats[0][0]
    for maxima, _ in stats[1:]:
        top = jnp.maximum(top, maxima)
    total = jnp.zeros_like(top)
    weights = []
    for maxima, sums in stats:
        factor = jnp.exp2((maxima - top) * EXP2_SCALE)
        total = total + factor * sums
        weights.append(factor.T)
    for p in range(PEERS):
        acc = jnp.zeros((HEADS * RPD, HD), jnp.float32)
        for part, weight in zip(sources, weights):
            value = part[p, :HEADS].astype(jnp.float32).reshape(HEADS * RPD, HD)
            acc = acc + value * weight[:, p : p + 1]
        out[p, :HEADS] = acc.reshape(HEADS, RPD, HD).astype(jnp.bfloat16)
    out[:, HEADS] = stats_tile(jnp.concatenate([top, total], axis=1))


def merge(parts):
    return pl.pallas_call(
        merge_kernel,
        in_specs=[VMEM] * len(parts),
        out_specs=VMEM,
        out_shape=jax.ShapeDtypeStruct((PEERS, BLK, RPD, HD), jnp.bfloat16),
        compiler_params=limit(8),
        name="merge",
    )(*parts)


def combine_kernel(parts, out):
    maxima, sums = read_stats(parts)
    top = jnp.max(maxima, axis=0, keepdims=True)
    factor = jnp.exp2((maxima - top) * EXP2_SCALE)
    denom = jnp.sum(factor * sums, axis=0, keepdims=True)
    weight = (factor / denom).T
    total = jnp.zeros((HEADS * RPD, HD), jnp.float32)
    for s in range(PEERS):
        block = parts[s, :HEADS].astype(jnp.float32).reshape(HEADS * RPD, HD)
        total = total + block * weight[:, s : s + 1]
    total = total.reshape(HEADS, RPD, HD)
    row = jnp.concatenate([total[h] for h in range(HEADS)], axis=1).astype(jnp.bfloat16)
    for s in range(PEERS):
        out[s] = row


def combine(parts):
    return pl.pallas_call(
        combine_kernel,
        in_specs=[VMEM],
        out_specs=VMEM,
        out_shape=jax.ShapeDtypeStruct((PEERS, RPD, HEADS * HD), jnp.bfloat16),
        compiler_params=limit(8),
        name="combine",
    )(parts)


def mix_kernel(core, rows, own, other, out):
    cols = own.shape[1]
    shape = (GROUPS, 1, ROWS // GROUPS, cols)
    flat = rows[...].reshape(ROWS, -1)
    for w, place in ((own, core[0]), (other, 1 - core[0])):
        part = jnp.dot(flat, w[...], preferred_element_type=jnp.float32)
        out[:, pl.ds(place, 1)] = part.reshape(shape).astype(jnp.bfloat16)


def mix(core, rows, own, other):
    return pl.pallas_call(
        mix_kernel,
        in_specs=[SMEM] + [VMEM] * 3,
        out_specs=VMEM,
        out_shape=jax.ShapeDtypeStruct((GROUPS, 2, ROWS // GROUPS, own.shape[1]), jnp.bfloat16),
        compiler_params=limit(8),
        name="mix",
    )(core, rows, own, other)


def swap_cores(x):
    return lax.ppermute(x, "core", [(0, 1), (1, 0)])


def exchange(x, axes):
    return lax.all_to_all(x, axes, split_axis=0, concat_axis=0, tiled=True)


def send_block(x, way):
    pairs = [
        (c * GROUPS + i, c * GROUPS + (i + (-way if c == 0 else way)) % GROUPS)
        for c in range(2)
        for i in range(GROUPS)
    ]
    return lax.ppermute(x, ("core", "head"), pairs)


def index_of(axis):
    return lax.axis_index(axis).astype(jnp.int32).reshape(1)


def shards(vision, w_key, w_value, queries, w_out):
    copies = jnp.broadcast_to(queries[None], (PEERS * GROUPS,) + queries.shape)
    rows = exchange(copies, YZX).reshape(PEERS, GROUPS, RPD, -1)
    kv1, twin = project(vision, w_key, w_value)
    kv2 = swap_cores(twin)
    head, core = index_of("head"), index_of("core")
    way = 2 * core - 1

    def attend_for(ahead):
        return attend((head + ahead + GROUPS) % GROUPS, rows, kv1, kv2)

    far = send_block(attend_for(2 * way), 1)
    back = send_block(attend_for(-way), -1)
    near = merge([attend_for(way), far])
    near = send_block(near, 1)
    part = merge([attend_for(0 * way), back, near])
    w_other = swap_cores(w_out)
    attended = exchange(combine(exchange(part, YZ)), YZ)
    partial = mix(core, attended, w_out, w_other)
    shape = partial.shape[2:]
    shares = exchange(partial.reshape((-1,) + shape), ("head", "core"))
    shares = shares.reshape(GROUPS, 2, GROUPS, RPD, -1).astype(jnp.float32)
    total = jnp.sum(shares, axis=0).transpose(1, 0, 2, 3)
    return total.reshape(2 * GROUPS * RPD, -1).astype(jnp.bfloat16)


def solution(mesh):
    fine = Mesh(mesh.devices.reshape(4, 4, 2, 4), ("y", "z", "core", "head"))
    seq = ("y", "z", "core")
    placed = (P(seq + ("head",), None), P(), P(), P(seq, "head"), P("head", seq))
    return jax.shard_map(
        shards, mesh=fine, in_specs=placed, out_specs=P("head", seq), check_vma=False
    )
```

```python
import math

import jax
import jax.numpy as jnp
from jax import lax
from jax.experimental import pallas as pl
from jax.experimental.pallas import tpu as pltpu
from jax.sharding import Mesh, PartitionSpec as P


HD = 128
GROUPS = 4
HEADS = 8
RPD = 8
PEERS = 16
ROWS = PEERS * RPD
STACK = 2
BLK = HEADS + 1
EXP2_SCALE = HD ** -0.5 * math.log2(math.e)
VMEM = pl.BlockSpec(memory_space=pltpu.VMEM)
HBM = pl.BlockSpec(memory_space=pltpu.HBM)
SMEM = pl.BlockSpec(memory_space=pltpu.SMEM)
YZ = ("y", "z")
CHUNKS = (768,) * 10
AHEAD = 3
AHEADS = (0, 0, 2, 1, -1)


def limit(mib):
    return pltpu.CompilerParams(vmem_limit_bytes=mib * 1024 * 1024)


def project_kernel(head, way, x, wk, wv, *rest):
    outs, (xb, wkb, wvb, acc, sems) = rest[: len(AHEADS)], rest[len(AHEADS) :]
    offsets = [sum(CHUNKS[:i]) for i in range(len(CHUNKS))]
    copies = []
    for i, (at, size) in enumerate(zip(offsets, CHUNKS)):
        part = pl.ds(at, size)
        copies.append(
            [
                pltpu.make_async_copy(x.at[:, part], xb.at[:, part], sems.at[0, i]),
                pltpu.make_async_copy(wk.at[part, :], wkb.at[part, :], sems.at[1, i]),
                pltpu.make_async_copy(wv.at[part, :], wvb.at[part, :], sems.at[2, i]),
            ]
        )
    for i in range(AHEAD):
        for copy in copies[i]:
            copy.start()
    last = len(CHUNKS) - 1
    for i, (at, size) in enumerate(zip(offsets, CHUNKS)):
        for copy in copies[i]:
            copy.wait()
        if i + AHEAD <= last:
            for copy in copies[i + AHEAD]:
                copy.start()
        for j, w in enumerate((wkb, wvb)):
            part = jnp.dot(
                xb[:, at : at + size], w[at : at + size, :], preferred_element_type=jnp.float32
            )
            if i > 0:
                part = acc[j] + part
            if i < last:
                acc[j] = part
            else:
                for g in range(GROUPS):
                    mine = part[:, g * HD : (g + 1) * HD].astype(jnp.bfloat16)
                    for ahead, out in zip(AHEADS, outs):

                        @pl.when((head[0] + ahead * way[0] + GROUPS) % GROUPS == g)
                        def _(out=out, mine=mine):
                            out[j] = mine


def project(head, way, vision, w_key, w_value):
    rows, width = vision.shape
    cols = w_key.shape[1]
    return pl.pallas_call(
        project_kernel,
        in_specs=[SMEM] * 2 + [HBM] * 3,
        out_specs=[VMEM] * len(AHEADS),
        out_shape=[pltpu.VMEM((2, rows, HD), jnp.bfloat16)]
        + [jax.ShapeDtypeStruct((2, rows, HD), jnp.bfloat16)] * GROUPS,
        scratch_shapes=[
            pltpu.VMEM((rows, width), jnp.bfloat16),
            pltpu.VMEM((width, cols), jnp.bfloat16),
            pltpu.VMEM((width, cols), jnp.bfloat16),
            pltpu.VMEM((2, rows, cols), jnp.float32),
            pltpu.SemaphoreType.DMA((3, len(CHUNKS))),
        ],
        compiler_params=limit(56),
        name="project",
    )(head, way, vision, w_key, w_value)


def stats_tile(stats):
    count = stats.shape[0]
    mine = stats.reshape(count, 1, HD)
    high = mine.astype(jnp.bfloat16).astype(jnp.float32)
    rest = mine - high
    mid = rest.astype(jnp.bfloat16).astype(jnp.float32)
    low = rest - mid
    place = lax.broadcasted_iota(jnp.int32, (count, RPD, HD), 1)
    tile = jnp.where(
        place == 0, high, jnp.where(place == 1, mid, jnp.where(place == 2, low, 0.0))
    )
    return tile.astype(jnp.bfloat16)


def attend_kernel(q, kv1, kv2, out):
    tokens = kv1.shape[1]
    row = lax.broadcasted_iota(jnp.int32, (ROWS, HD), 0)
    lane = lax.broadcasted_iota(jnp.int32, (ROWS, HD), 1)
    contract = (((1,), (1,)), ((), ()))
    ones = jnp.ones((tokens, HD), jnp.bfloat16)
    k1, k2 = kv1[0], kv2[0]
    v1 = jnp.concatenate([kv1[1], ones], axis=1)
    v2 = jnp.concatenate([kv2[1], ones], axis=1)
    stats = jnp.zeros((ROWS, HD), jnp.float32)
    for first in range(0, HEADS, STACK):
        qs = [
            q[:, :, h * HD : (h + 1) * HD].reshape(ROWS, HD)
            for h in range(first, first + STACK)
        ]
        qs = jnp.concatenate(qs, axis=0)
        s1 = lax.dot_general(qs, k1, contract, preferred_element_type=jnp.float32)
        s2 = lax.dot_general(qs, k2, contract, preferred_element_type=jnp.float32)
        top = jnp.max(jnp.maximum(s1, s2), axis=1, keepdims=True)
        p1 = jnp.exp2((s1 - top) * EXP2_SCALE).astype(jnp.bfloat16)
        p2 = jnp.exp2((s2 - top) * EXP2_SCALE).astype(jnp.bfloat16)
        acc = jnp.dot(p1, v1, preferred_element_type=jnp.float32) + jnp.dot(
            p2, v2, preferred_element_type=jnp.float32
        )
        for k in range(STACK):
            h = first + k
            mine = acc[k * ROWS : (k + 1) * ROWS]
            out[:, h] = mine[:, :HD].reshape(PEERS, RPD, HD).astype(jnp.bfloat16)
            pair = h * RPD + row % RPD
            stats = jnp.where(lane == pair, top[k * ROWS : (k + 1) * ROWS], stats)
            stats = jnp.where(lane == HD // 2 + pair, mine[:, HD:], stats)
    out[:, HEADS] = stats_tile(jnp.sum(stats.reshape(PEERS, RPD, HD), axis=1))


def attend(q, kv1, kv2):
    return pl.pallas_call(
        attend_kernel,
        in_specs=[VMEM] * 3,
        out_specs=VMEM,
        out_shape=jax.ShapeDtypeStruct((PEERS, BLK, RPD, HD), jnp.bfloat16),
        compiler_params=limit(24),
        name="attend",
    )(q, kv1, kv2)


def read_stats(part):
    stats = jnp.sum(part[:, HEADS].astype(jnp.float32), axis=1)
    return stats[:, : HD // 2], stats[:, HD // 2 :]


def merge_kernel(*refs):
    sources, out = refs[:-1], refs[-1]
    stats = [read_stats(part) for part in sources]
    top = stats[0][0]
    for maxima, _ in stats[1:]:
        top = jnp.maximum(top, maxima)
    total = jnp.zeros_like(top)
    weights = []
    for maxima, sums in stats:
        factor = jnp.exp2((maxima - top) * EXP2_SCALE)
        total = total + factor * sums
        weights.append(factor.T)
    for p in range(PEERS):
        acc = jnp.zeros((HEADS * RPD, HD), jnp.float32)
        for part, weight in zip(sources, weights):
            value = part[p, :HEADS].astype(jnp.float32).reshape(HEADS * RPD, HD)
            acc = acc + value * weight[:, p : p + 1]
        out[p, :HEADS] = acc.reshape(HEADS, RPD, HD).astype(jnp.bfloat16)
    out[:, HEADS] = stats_tile(jnp.concatenate([top, total], axis=1))


def merge(parts):
    return pl.pallas_call(
        merge_kernel,
        in_specs=[VMEM] * len(parts),
        out_specs=VMEM,
        out_shape=jax.ShapeDtypeStruct((PEERS, BLK, RPD, HD), jnp.bfloat16),
        compiler_params=limit(8),
        name="merge",
    )(*parts)


def combine_kernel(parts, out):
    maxima, sums = read_stats(parts)
    top = jnp.max(maxima, axis=0, keepdims=True)
    factor = jnp.exp2((maxima - top) * EXP2_SCALE)
    denom = jnp.sum(factor * sums, axis=0, keepdims=True)
    weight = (factor / denom).T
    total = jnp.zeros((HEADS * RPD, HD), jnp.float32)
    for s in range(PEERS):
        block = parts[s, :HEADS].astype(jnp.float32).reshape(HEADS * RPD, HD)
        total = total + block * weight[:, s : s + 1]
    total = total.reshape(HEADS, RPD, HD)
    row = jnp.concatenate([total[h] for h in range(HEADS)], axis=1).astype(jnp.bfloat16)
    for s in range(PEERS):
        out[s] = row


def combine(parts):
    return pl.pallas_call(
        combine_kernel,
        in_specs=[VMEM],
        out_specs=VMEM,
        out_shape=jax.ShapeDtypeStruct((PEERS, RPD, HEADS * HD), jnp.bfloat16),
        compiler_params=limit(8),
        name="combine",
    )(parts)


def mix_kernel(core, rows, own, other, out):
    cols = own.shape[1]
    shape = (GROUPS, 1, ROWS // GROUPS, cols)
    flat = rows[...].reshape(ROWS, -1)
    for w, place in ((own, core[0]), (other, 1 - core[0])):
        part = jnp.dot(flat, w[...], preferred_element_type=jnp.float32)
        out[:, pl.ds(place, 1)] = part.reshape(shape).astype(jnp.bfloat16)


def mix(core, rows, own, other):
    return pl.pallas_call(
        mix_kernel,
        in_specs=[SMEM] + [VMEM] * 3,
        out_specs=VMEM,
        out_shape=jax.ShapeDtypeStruct((GROUPS, 2, ROWS // GROUPS, own.shape[1]), jnp.bfloat16),
        compiler_params=limit(8),
        name="mix",
    )(core, rows, own, other)


def swap_cores(x):
    return lax.ppermute(x, "core", [(0, 1), (1, 0)])


def exchange(x, axes):
    return lax.all_to_all(x, axes, split_axis=0, concat_axis=0, tiled=True)


def send_block(x, way):
    pairs = [
        (c * GROUPS + i, c * GROUPS + (i + (-way if c == 0 else way)) % GROUPS)
        for c in range(2)
        for i in range(GROUPS)
    ]
    return lax.ppermute(x, ("core", "head"), pairs)


def index_of(axis):
    return lax.axis_index(axis).astype(jnp.int32).reshape(1)


def shards(vision, w_key, w_value, queries, w_out):
    copies = jnp.broadcast_to(queries[None], (PEERS,) + queries.shape)
    rows = exchange(copies, YZ)
    head, core = index_of("head"), index_of("core")
    own, twin, far, near, back = project(head, 2 * core - 1, vision, w_key, w_value)
    far = send_block(far, 2)
    near = send_block(near, 1)
    back = send_block(back, -1)
    parts = [
        attend(rows, kv, swap_cores(sent))
        for kv, sent in ((own, twin), (near, near), (back, back), (far, far))
    ]
    part = merge(parts)
    w_other = swap_cores(w_out)
    attended = exchange(combine(exchange(part, YZ)), YZ)
    partial = mix(core, attended, w_out, w_other)
    shape = partial.shape[2:]
    shares = exchange(partial.reshape((-1,) + shape), ("head", "core"))
    shares = shares.reshape(GROUPS, 2, GROUPS, RPD, -1).astype(jnp.float32)
    total = jnp.sum(shares, axis=0).transpose(1, 0, 2, 3)
    return total.reshape(2 * GROUPS * RPD, -1).astype(jnp.bfloat16)


def solution(mesh):
    fine = Mesh(mesh.devices.reshape(4, 4, 2, 4), ("y", "z", "core", "head"))
    seq = ("y", "z", "core")
    placed = (P(seq + ("head",), None), P(), P(), P(seq, "head"), P("head", seq))
    return jax.shard_map(
        shards, mesh=fine, in_specs=placed, out_specs=P("head", seq), check_vma=False
    )
```

```python
import math

import jax
import jax.numpy as jnp
from jax import lax
from jax.experimental import pallas as pl
from jax.experimental.pallas import tpu as pltpu
from jax.sharding import Mesh, PartitionSpec as P


HD = 128
GROUPS = 4
HEADS = 8
RPD = 8
PEERS = 16
ROWS = PEERS * RPD
STACK = 2
BLK = HEADS + 1
EXP2_SCALE = HD ** -0.5 * math.log2(math.e)
VMEM = pl.BlockSpec(memory_space=pltpu.VMEM)
HBM = pl.BlockSpec(memory_space=pltpu.HBM)
SMEM = pl.BlockSpec(memory_space=pltpu.SMEM)
YZ = ("y", "z")
CHUNKS = (768,) * 10
AHEAD = 3
AHEADS = (0, 2, 1, -1)


def limit(mib):
    return pltpu.CompilerParams(vmem_limit_bytes=mib * 1024 * 1024)


def project_kernel(head, way, x, wk, wv, *rest):
    outs, (xb, wkb, wvb, acc, sems) = rest[: len(AHEADS)], rest[len(AHEADS) :]
    offsets = [sum(CHUNKS[:i]) for i in range(len(CHUNKS))]
    copies = []
    for i, (at, size) in enumerate(zip(offsets, CHUNKS)):
        part = pl.ds(at, size)
        copies.append(
            [
                pltpu.make_async_copy(x.at[:, part], xb.at[:, part], sems.at[0, i]),
                pltpu.make_async_copy(wk.at[part, :], wkb.at[part, :], sems.at[1, i]),
                pltpu.make_async_copy(wv.at[part, :], wvb.at[part, :], sems.at[2, i]),
            ]
        )
    for i in range(AHEAD):
        for copy in copies[i]:
            copy.start()
    last = len(CHUNKS) - 1
    for i, (at, size) in enumerate(zip(offsets, CHUNKS)):
        for copy in copies[i]:
            copy.wait()
        if i + AHEAD <= last:
            for copy in copies[i + AHEAD]:
                copy.start()
        for j, w in enumerate((wkb, wvb)):
            part = jnp.dot(
                xb[:, at : at + size], w[at : at + size, :], preferred_element_type=jnp.float32
            )
            if i > 0:
                part = acc[j] + part
            if i < last:
                acc[j] = part
            else:
                for g in range(GROUPS):
                    mine = part[:, g * HD : (g + 1) * HD].astype(jnp.bfloat16)
                    for ahead, out in zip(AHEADS, outs):

                        @pl.when((head[0] + ahead * way[0] + GROUPS) % GROUPS == g)
                        def _(out=out, mine=mine):
                            out[j] = mine


def project(head, way, vision, w_key, w_value):
    rows, width = vision.shape
    cols = w_key.shape[1]
    return pl.pallas_call(
        project_kernel,
        in_specs=[SMEM] * 2 + [HBM] * 3,
        out_specs=[VMEM] * len(AHEADS),
        out_shape=[pltpu.VMEM((2, rows, HD), jnp.bfloat16)] * len(AHEADS),
        scratch_shapes=[
            pltpu.VMEM((rows, width), jnp.bfloat16),
            pltpu.VMEM((width, cols), jnp.bfloat16),
            pltpu.VMEM((width, cols), jnp.bfloat16),
            pltpu.VMEM((2, rows, cols), jnp.float32),
            pltpu.SemaphoreType.DMA((3, len(CHUNKS))),
        ],
        compiler_params=limit(56),
        name="project",
    )(head, way, vision, w_key, w_value)


def stats_tile(stats):
    count = stats.shape[0]
    mine = stats.reshape(count, 1, HD)
    high = mine.astype(jnp.bfloat16).astype(jnp.float32)
    rest = mine - high
    mid = rest.astype(jnp.bfloat16).astype(jnp.float32)
    low = rest - mid
    place = lax.broadcasted_iota(jnp.int32, (count, RPD, HD), 1)
    tile = jnp.where(
        place == 0, high, jnp.where(place == 1, mid, jnp.where(place == 2, low, 0.0))
    )
    return tile.astype(jnp.bfloat16)


def attend_kernel(q, *rest):
    kvs, out = rest[:-1], rest[-1]
    row = lax.broadcasted_iota(jnp.int32, (ROWS, HD), 0)
    lane = lax.broadcasted_iota(jnp.int32, (ROWS, HD), 1)
    contract = (((1,), (1,)), ((), ()))
    ones = jnp.ones(kvs[0].shape[1:], jnp.bfloat16)
    values = [jnp.concatenate([kv[1], ones], axis=1) for kv in kvs]
    stats = jnp.zeros((ROWS, HD), jnp.float32)
    for first in range(0, HEADS, STACK):
        qs = [
            q[:, :, h * HD : (h + 1) * HD].reshape(ROWS, HD) for h in range(first, first + STACK)
        ]
        qs = jnp.concatenate(qs, axis=0)
        scores = [
            lax.dot_general(qs, kv[0], contract, preferred_element_type=jnp.float32)
            for kv in kvs
        ]
        top = scores[0]
        for s in scores[1:]:
            top = jnp.maximum(top, s)
        top = jnp.max(top, axis=1, keepdims=True)
        acc = jnp.zeros((STACK * ROWS, 2 * HD), jnp.float32)
        for s, v in zip(scores, values):
            p = jnp.exp2((s - top) * EXP2_SCALE).astype(jnp.bfloat16)
            acc = acc + jnp.dot(p, v, preferred_element_type=jnp.float32)
        for k in range(STACK):
            h = first + k
            mine = acc[k * ROWS : (k + 1) * ROWS]
            out[:, h] = mine[:, :HD].reshape(PEERS, RPD, HD).astype(jnp.bfloat16)
            pair = h * RPD + row % RPD
            stats = jnp.where(lane == pair, top[k * ROWS : (k + 1) * ROWS], stats)
            stats = jnp.where(lane == HD // 2 + pair, mine[:, HD:], stats)
    out[:, HEADS] = stats_tile(jnp.sum(stats.reshape(PEERS, RPD, HD), axis=1))


def attend(q, kvs):
    return pl.pallas_call(
        attend_kernel,
        in_specs=[VMEM] * (1 + len(kvs)),
        out_specs=VMEM,
        out_shape=jax.ShapeDtypeStruct((PEERS, BLK, RPD, HD), jnp.bfloat16),
        compiler_params=limit(40),
        name="attend",
    )(q, *kvs)


def read_stats(part):
    stats = jnp.sum(part[:, HEADS].astype(jnp.float32), axis=1)
    return stats[:, : HD // 2], stats[:, HD // 2 :]


def merge_kernel(*refs):
    sources, out = refs[:-1], refs[-1]
    stats = [read_stats(part) for part in sources]
    top = stats[0][0]
    for maxima, _ in stats[1:]:
        top = jnp.maximum(top, maxima)
    total = jnp.zeros_like(top)
    weights = []
    for maxima, sums in stats:
        factor = jnp.exp2((maxima - top) * EXP2_SCALE)
        total = total + factor * sums
        weights.append(factor.T)
    for p in range(PEERS):
        acc = jnp.zeros((HEADS * RPD, HD), jnp.float32)
        for part, weight in zip(sources, weights):
            value = part[p, :HEADS].astype(jnp.float32).reshape(HEADS * RPD, HD)
            acc = acc + value * weight[:, p : p + 1]
        out[p, :HEADS] = acc.reshape(HEADS, RPD, HD).astype(jnp.bfloat16)
    out[:, HEADS] = stats_tile(jnp.concatenate([top, total], axis=1))


def merge(parts):
    return pl.pallas_call(
        merge_kernel,
        in_specs=[VMEM] * len(parts),
        out_specs=VMEM,
        out_shape=jax.ShapeDtypeStruct((PEERS, BLK, RPD, HD), jnp.bfloat16),
        compiler_params=limit(8),
        name="merge",
    )(*parts)


def combine_kernel(parts, out):
    maxima, sums = read_stats(parts)
    top = jnp.max(maxima, axis=0, keepdims=True)
    factor = jnp.exp2((maxima - top) * EXP2_SCALE)
    denom = jnp.sum(factor * sums, axis=0, keepdims=True)
    weight = (factor / denom).T
    total = jnp.zeros((HEADS * RPD, HD), jnp.float32)
    for s in range(PEERS):
        block = parts[s, :HEADS].astype(jnp.float32).reshape(HEADS * RPD, HD)
        total = total + block * weight[:, s : s + 1]
    total = total.reshape(HEADS, RPD, HD)
    row = jnp.concatenate([total[h] for h in range(HEADS)], axis=1).astype(jnp.bfloat16)
    for s in range(PEERS):
        out[s] = row


def combine(parts):
    return pl.pallas_call(
        combine_kernel,
        in_specs=[VMEM],
        out_specs=VMEM,
        out_shape=jax.ShapeDtypeStruct((PEERS, RPD, HEADS * HD), jnp.bfloat16),
        compiler_params=limit(8),
        name="combine",
    )(parts)


def mix_kernel(core, rows, own, other, out):
    cols = own.shape[1]
    shape = (GROUPS, 1, ROWS // GROUPS, cols)
    flat = rows[...].reshape(ROWS, -1)
    for w, place in ((own, core[0]), (other, 1 - core[0])):
        part = jnp.dot(flat, w[...], preferred_element_type=jnp.float32)
        out[:, pl.ds(place, 1)] = part.reshape(shape).astype(jnp.bfloat16)


def mix(core, rows, own, other):
    return pl.pallas_call(
        mix_kernel,
        in_specs=[SMEM] + [VMEM] * 3,
        out_specs=VMEM,
        out_shape=jax.ShapeDtypeStruct((GROUPS, 2, ROWS // GROUPS, own.shape[1]), jnp.bfloat16),
        compiler_params=limit(8),
        name="mix",
    )(core, rows, own, other)


def total_kernel(shares, out):
    total = shares[0].astype(jnp.float32)
    for g in range(1, GROUPS):
        total = total + shares[g].astype(jnp.float32)
    cols = out.shape[1]
    total = total.reshape(2, GROUPS, RPD, cols)
    pair = jnp.concatenate([total[0][:, None], total[1][:, None]], axis=1)
    out[...] = pair.reshape(2 * GROUPS * RPD, cols).astype(jnp.bfloat16)


def total_of(shares):
    rows, cols = shares.shape[1:]
    return pl.pallas_call(
        total_kernel,
        in_specs=[VMEM],
        out_specs=VMEM,
        out_shape=jax.ShapeDtypeStruct((rows, cols), jnp.bfloat16),
        compiler_params=limit(4),
        name="total",
    )(shares)


def swap_cores(x):
    return lax.ppermute(x, "core", [(0, 1), (1, 0)])


def exchange(x, axes):
    return lax.all_to_all(x, axes, split_axis=0, concat_axis=0, tiled=True)


def send_block(x, way):
    pairs = [
        (c * GROUPS + i, c * GROUPS + (i + (-way if c == 0 else way)) % GROUPS)
        for c in range(2)
        for i in range(GROUPS)
    ]
    return lax.ppermute(x, ("core", "head"), pairs)


def index_of(axis):
    return lax.axis_index(axis).astype(jnp.int32).reshape(1)


def shards(vision, w_key, w_value, queries, w_out):
    copies = jnp.broadcast_to(queries[None], (PEERS,) + queries.shape)
    rows = exchange(copies, YZ)
    head, core = index_of("head"), index_of("core")
    own, far, near, back = project(head, 2 * core - 1, vision, w_key, w_value)
    far = send_block(far, 2)
    near = send_block(near, 1)
    back = send_block(back, -1)
    part_own = attend(rows, [own, swap_cores(own)])
    others = [near, back, far]
    others += [swap_cores(near), swap_cores(back), swap_cores(far)]
    part = merge([part_own, attend(rows, others)])
    w_other = swap_cores(w_out)
    attended = exchange(combine(exchange(part, YZ)), YZ)
    partial = mix(core, attended, w_out, w_other)
    shape = partial.shape[2:]
    shares = exchange(partial.reshape((-1,) + shape), ("head", "core"))
    return total_of(shares.reshape(GROUPS, 2 * GROUPS * RPD, -1))


def solution(mesh):
    fine = Mesh(mesh.devices.reshape(4, 4, 2, 4), ("y", "z", "core", "head"))
    seq = ("y", "z", "core")
    placed = (P(seq + ("head",), None), P(), P(), P(seq, "head"), P("head", seq))
    return jax.shard_map(
        shards, mesh=fine, in_specs=placed, out_specs=P("head", seq), check_vma=False
    )
```

```python
import math

import jax
import jax.numpy as jnp
from jax import lax
from jax.experimental import pallas as pl
from jax.experimental.pallas import tpu as pltpu
from jax.sharding import Mesh, PartitionSpec as P


HD = 128
GROUPS = 4
HEADS = 8
RPD = 8
PEERS = 16
ROWS = PEERS * RPD
STACK = 2
BLK = HEADS + 1
EXP2_SCALE = HD ** -0.5 * math.log2(math.e)
VMEM = pl.BlockSpec(memory_space=pltpu.VMEM)
HBM = pl.BlockSpec(memory_space=pltpu.HBM)
SMEM = pl.BlockSpec(memory_space=pltpu.SMEM)
YZ = ("y", "z")
CHUNKS = (768,) * 10
AHEAD = 10
AHEADS = (0, 2, 1, -1)


def limit(mib):
    return pltpu.CompilerParams(vmem_limit_bytes=mib * 1024 * 1024)


def project_kernel(head, way, x, wk, wv, *rest):
    outs, (xb, wkb, wvb, acc, sems) = rest[: len(AHEADS)], rest[len(AHEADS) :]
    offsets = [sum(CHUNKS[:i]) for i in range(len(CHUNKS))]
    copies = []
    for i, (at, size) in enumerate(zip(offsets, CHUNKS)):
        part = pl.ds(at, size)
        copies.append(
            [
                pltpu.make_async_copy(x.at[:, part], xb.at[:, part], sems.at[0, i]),
                pltpu.make_async_copy(wk.at[part, :], wkb.at[part, :], sems.at[1, i]),
                pltpu.make_async_copy(wv.at[part, :], wvb.at[part, :], sems.at[2, i]),
            ]
        )
    for i in range(AHEAD):
        for copy in copies[i]:
            copy.start()
    last = len(CHUNKS) - 1
    for i, (at, size) in enumerate(zip(offsets, CHUNKS)):
        for copy in copies[i]:
            copy.wait()
        if i + AHEAD <= last:
            for copy in copies[i + AHEAD]:
                copy.start()
        for j, w in enumerate((wkb, wvb)):
            part = jnp.dot(
                xb[:, at : at + size], w[at : at + size, :], preferred_element_type=jnp.float32
            )
            if i > 0:
                part = acc[j] + part
            if i < last:
                acc[j] = part
            else:
                for g in range(GROUPS):
                    mine = part[:, g * HD : (g + 1) * HD].astype(jnp.bfloat16)
                    for ahead, out in zip(AHEADS, outs):

                        @pl.when((head[0] + ahead * way[0] + GROUPS) % GROUPS == g)
                        def _(out=out, mine=mine):
                            out[j] = mine


def project(head, way, vision, w_key, w_value):
    rows, width = vision.shape
    cols = w_key.shape[1]
    return pl.pallas_call(
        project_kernel,
        in_specs=[SMEM] * 2 + [HBM] * 3,
        out_specs=[VMEM] * len(AHEADS),
        out_shape=[pltpu.VMEM((2, rows, HD), jnp.bfloat16)] * len(AHEADS),
        scratch_shapes=[
            pltpu.VMEM((rows, width), jnp.bfloat16),
            pltpu.VMEM((width, cols), jnp.bfloat16),
            pltpu.VMEM((width, cols), jnp.bfloat16),
            pltpu.VMEM((2, rows, cols), jnp.float32),
            pltpu.SemaphoreType.DMA((3, len(CHUNKS))),
        ],
        compiler_params=limit(56),
        name="project",
    )(head, way, vision, w_key, w_value)


def stats_tile(stats):
    count = stats.shape[0]
    mine = stats.reshape(count, 1, HD)
    high = mine.astype(jnp.bfloat16).astype(jnp.float32)
    rest = mine - high
    mid = rest.astype(jnp.bfloat16).astype(jnp.float32)
    low = rest - mid
    place = lax.broadcasted_iota(jnp.int32, (count, RPD, HD), 1)
    tile = jnp.where(
        place == 0, high, jnp.where(place == 1, mid, jnp.where(place == 2, low, 0.0))
    )
    return tile.astype(jnp.bfloat16)


def attend_heads(q, kvs, first):
    contract = (((1,), (1,)), ((), ()))
    qs = [q[:, :, h * HD : (h + 1) * HD].reshape(ROWS, HD) for h in range(first, first + STACK)]
    qs = jnp.concatenate(qs, axis=0)
    scores = [
        lax.dot_general(qs, kv[0], contract, preferred_element_type=jnp.float32) for kv in kvs
    ]
    top = scores[0]
    for s in scores[1:]:
        top = jnp.maximum(top, s)
    return scores, jnp.max(top, axis=1, keepdims=True)


def weigh(scores, values, top, acc):
    for s, v in zip(scores, values):
        p = jnp.exp2((s - top) * EXP2_SCALE).astype(jnp.bfloat16)
        acc = acc + jnp.dot(p, v, preferred_element_type=jnp.float32)
    return acc


def with_ones(kvs):
    ones = jnp.ones(kvs[0].shape[1:], jnp.bfloat16)
    return [jnp.concatenate([kv[1], ones], axis=1) for kv in kvs]


def begin_kernel(q, *rest):
    kvs, out = rest[:-1], rest[-1]
    values = with_ones(kvs)
    shape = (STACK * ROWS, 2 * HD)
    lane = lax.broadcasted_iota(jnp.int32, shape, 1)
    for first in range(0, HEADS, STACK):
        scores, top = attend_heads(q, kvs, first)
        acc = weigh(scores, values, top, jnp.zeros(shape, jnp.float32))
        out[first * ROWS : (first + STACK) * ROWS, :] = jnp.where(lane == 2 * HD - 1, top, acc)


def finish_kernel(q, begun, *rest):
    kvs, out = rest[:-1], rest[-1]
    values = with_ones(kvs)
    row = lax.broadcasted_iota(jnp.int32, (ROWS, HD), 0)
    lane = lax.broadcasted_iota(jnp.int32, (ROWS, HD), 1)
    stats = jnp.zeros((ROWS, HD), jnp.float32)
    for first in range(0, HEADS, STACK):
        before = begun[first * ROWS : (first + STACK) * ROWS, :]
        top_before = before[:, 2 * HD - 1 :]
        scores, top = attend_heads(q, kvs, first)
        top = jnp.maximum(top, top_before)
        acc = before * jnp.exp2((top_before - top) * EXP2_SCALE)
        acc = weigh(scores, values, top, acc)
        for k in range(STACK):
            h = first + k
            mine = acc[k * ROWS : (k + 1) * ROWS]
            sums = mine[:, HD : HD + 1]
            out[:, h] = mine[:, :HD].reshape(PEERS, RPD, HD).astype(jnp.bfloat16)
            pair = h * RPD + row % RPD
            stats = jnp.where(lane == pair, top[k * ROWS : (k + 1) * ROWS], stats)
            stats = jnp.where(lane == HD // 2 + pair, sums, stats)
    out[:, HEADS] = stats_tile(jnp.sum(stats.reshape(PEERS, RPD, HD), axis=1))


def attend(kernel, out_shape, q, arrays):
    return pl.pallas_call(
        kernel,
        in_specs=[VMEM] * (1 + len(arrays)),
        out_specs=VMEM,
        out_shape=out_shape,
        compiler_params=limit(40),
        name="attend",
    )(q, *arrays)


def read_stats(part):
    stats = jnp.sum(part[:, HEADS].astype(jnp.float32), axis=1)
    return stats[:, : HD // 2], stats[:, HD // 2 :]


def combine_kernel(parts, out):
    maxima, sums = read_stats(parts)
    top = jnp.max(maxima, axis=0, keepdims=True)
    factor = jnp.exp2((maxima - top) * EXP2_SCALE)
    denom = jnp.sum(factor * sums, axis=0, keepdims=True)
    weight = (factor / denom).T
    total = jnp.zeros((HEADS * RPD, HD), jnp.float32)
    for s in range(PEERS):
        block = parts[s, :HEADS].astype(jnp.float32).reshape(HEADS * RPD, HD)
        total = total + block * weight[:, s : s + 1]
    total = total.reshape(HEADS, RPD, HD)
    row = jnp.concatenate([total[h] for h in range(HEADS)], axis=1).astype(jnp.bfloat16)
    for s in range(PEERS):
        out[s] = row


def combine(parts):
    return pl.pallas_call(
        combine_kernel,
        in_specs=[VMEM],
        out_specs=VMEM,
        out_shape=jax.ShapeDtypeStruct((PEERS, RPD, HEADS * HD), jnp.bfloat16),
        compiler_params=limit(8),
        name="combine",
    )(parts)


def mix_kernel(core, rows, own, other, out):
    cols = own.shape[1]
    shape = (GROUPS, 1, ROWS // GROUPS, cols)
    flat = rows[...].reshape(ROWS, -1)
    for w, place in ((own, core[0]), (other, 1 - core[0])):
        part = jnp.dot(flat, w[...], preferred_element_type=jnp.float32)
        out[:, pl.ds(place, 1)] = part.reshape(shape).astype(jnp.bfloat16)


def mix(core, rows, own, other):
    return pl.pallas_call(
        mix_kernel,
        in_specs=[SMEM] + [VMEM] * 3,
        out_specs=VMEM,
        out_shape=jax.ShapeDtypeStruct((GROUPS, 2, ROWS // GROUPS, own.shape[1]), jnp.bfloat16),
        compiler_params=limit(8),
        name="mix",
    )(core, rows, own, other)


def total_kernel(shares, out):
    total = shares[0].astype(jnp.float32)
    for g in range(1, GROUPS):
        total = total + shares[g].astype(jnp.float32)
    cols = out.shape[1]
    total = total.reshape(2, GROUPS, RPD, cols)
    pair = jnp.concatenate([total[0][:, None], total[1][:, None]], axis=1)
    out[...] = pair.reshape(2 * GROUPS * RPD, cols).astype(jnp.bfloat16)


def total_of(shares):
    rows, cols = shares.shape[1:]
    return pl.pallas_call(
        total_kernel,
        in_specs=[VMEM],
        out_specs=VMEM,
        out_shape=jax.ShapeDtypeStruct((rows, cols), jnp.bfloat16),
        compiler_params=limit(4),
        name="total",
    )(shares)


def swap_cores(x):
    return lax.ppermute(x, "core", [(0, 1), (1, 0)])


def exchange(x, axes):
    return lax.all_to_all(x, axes, split_axis=0, concat_axis=0, tiled=True)


def send_block(x, way):
    pairs = [
        (c * GROUPS + i, c * GROUPS + (i + (-way if c == 0 else way)) % GROUPS)
        for c in range(2)
        for i in range(GROUPS)
    ]
    return lax.ppermute(x, ("core", "head"), pairs)


def index_of(axis):
    return lax.axis_index(axis).astype(jnp.int32).reshape(1)


def shards(vision, w_key, w_value, queries, w_out):
    copies = jnp.broadcast_to(queries[None], (PEERS,) + queries.shape)
    rows = exchange(copies, YZ)
    head, core = index_of("head"), index_of("core")
    own, far, near, back = project(head, 2 * core - 1, vision, w_key, w_value)
    far = send_block(far, 2)
    near = send_block(near, 1)
    back = send_block(back, -1)
    begun = jax.ShapeDtypeStruct((HEADS * ROWS, 2 * HD), jnp.float32)
    begun = attend(begin_kernel, begun, rows, [own, swap_cores(own)])
    others = [near, back, far]
    others += [swap_cores(near), swap_cores(back), swap_cores(far)]
    shape = jax.ShapeDtypeStruct((PEERS, BLK, RPD, HD), jnp.bfloat16)
    part = attend(finish_kernel, shape, rows, [begun] + others)
    w_other = swap_cores(w_out)
    attended = exchange(combine(exchange(part, YZ)), YZ)
    partial = mix(core, attended, w_out, w_other)
    shape = partial.shape[2:]
    shares = exchange(partial.reshape((-1,) + shape), ("head", "core"))
    return total_of(shares.reshape(GROUPS, 2 * GROUPS * RPD, -1))


def solution(mesh):
    fine = Mesh(mesh.devices.reshape(4, 4, 2, 4), ("y", "z", "core", "head"))
    seq = ("y", "z", "core")
    placed = (P(seq + ("head",), None), P(), P(), P(seq, "head"), P("head", seq))
    return jax.shard_map(
        shards, mesh=fine, in_specs=placed, out_specs=P("head", seq), check_vma=False
    )
```
